256 devices in a mesh: freq: 4 (over x_lo, core), rcv: 64 (over y, x_hi, z).
Axes of the slice: x: 4 (x_hi: 2, x_lo: 2; x = x_hi * 2 + x_lo), y: 4, z: 8, core: 2. Of those that a mesh axis runs over, the one named last changes fastest.
Arguments:
- spectra: bfloat16 [2, 128, 384, 8192], P(None, None, 'freq', 'rcv'), may hold values from -600 to 600
- valid: int32 [384, 8192], P(None, 'rcv'), may hold values from 0 to 1, as said below
- sources: int32 [256], P('rcv'), may hold values from 0 to 8191, as said below
- bounds: int32 [256, 8192, 2], P('freq', 'rcv'), may hold values from 0 to 128, as said below
Outputs:
- lag_corr: bfloat16 [256, 8192, 128], P('freq', 'rcv')
- peak_value: float32 [256, 8192], P('freq', 'rcv')
The draws below stay inside these ranges and needn't reach their ends.
Inputs may be any that keep to these rules, and one draw needn't show every extreme that they name: `valid`: in each aligned group of 4 sub-windows at most one entry of a channel is 0. Source s is a channel from (s // 4) * 128 to (s // 4 + 1) * 128 - 1; the sources are distinct. bounds[s, c, 0] < bounds[s, c, 1] <= 128, and the window holds 16 to 64 lag samples.
All inputs are finite; a program needn't handle non-finite values.
Results may differ from the reference program's by a relative error of at most 0.007.
Values may be sent and summed in bfloat16 or wider, within the bound.
No kernel may reach another device: no remote copies, remote signals or barrier semaphores. Data moves between devices by JAX's collectives and lax.ppermute only.
A program may use at most 128 MiB of HBM per device.

```python
import math
import jax
import jax.numpy as jnp
from jax import lax

F = 128
L = 128
W = 384
CH_DEV = 128
SRC_DEV = 4
S = 256
C = 8192


def draw_spectra(key, part):
    subkeys = jax.random.split(key, 3)
    row_scale = jnp.exp(jax.random.uniform(subkeys[0], (1, 1, W, C), minval=0.0, maxval=math.log(10.0)))
    bin_scale = jnp.exp(jax.random.uniform(subkeys[1], (1, F, 1, 1), minval=0.0, maxval=math.log(10.0)))
    values = jnp.clip(jax.random.normal(subkeys[2], (2, F, W, C), dtype=jnp.float32), -6.0, 6.0)
    return (values * row_scale * bin_scale).astype(jnp.bfloat16)


def draw_valid(key, part):
    dropped = jax.random.randint(key, (W // 4, 1, C), 0, 5)
    within = jnp.arange(4, dtype=jnp.int32)[None, :, None]
    return (within != dropped).astype(jnp.int32).reshape(W, C)


def draw_sources(key, part):
    blocks = S // SRC_DEV
    scores = jax.random.randint(key, (blocks, CH_DEV), 0, 2 ** 20) * CH_DEV + jnp.arange(CH_DEV, dtype=jnp.int32)[None, :]
    scores = scores.at[0, 0].set(-2)
    scores = scores.at[blocks - 1, CH_DEV - 1].set(-1)
    chosen = jnp.argsort(scores, axis=1)[:, :SRC_DEV].astype(jnp.int32)
    offsets = jnp.arange(blocks, dtype=jnp.int32)[:, None] * CH_DEV
    return (offsets + chosen).reshape(S).astype(jnp.int32)


def draw_bounds(key, part):
    subkeys = jax.random.split(key, 2)
    widths = jax.random.randint(subkeys[0], (S, C, 1), L // 8, L // 2 + 1)
    lower = jax.random.randint(subkeys[1], (S, C, 1), 0, L - widths + 1)
    return jnp.concatenate([lower, lower + widths], axis=2).astype(jnp.int32)


def setup_inputs(seed: int = 0) -> dict:
    keys = jax.random.split(jax.random.key(seed), 5)
    spectra = draw_spectra(jax.random.fold_in(keys[4], 71), 0)
    valid = draw_valid(jax.random.fold_in(keys[4], 71), 0)
    sources = draw_sources(jax.random.fold_in(keys[4], 71), 0)
    bounds = draw_bounds(jax.random.fold_in(keys[4], 71), 0)
    return {"spectra": spectra, "valid": valid, "sources": sources, "bounds": bounds}


def whiten(block, valid_block):
    spectra_f = block.astype(jnp.float32)
    energy = lax.optimization_barrier(jnp.mean(spectra_f[0] * spectra_f[0] + spectra_f[1] * spectra_f[1], axis=0))
    scaling = valid_block.astype(jnp.float32) / jnp.sqrt(energy + 1e-06)
    return (spectra_f * scaling).astype(jnp.bfloat16)

def make_tables(bin_first, bin_count, lag_count, period):
    bins_col = (bin_first + 1 + jnp.arange(bin_count, dtype=jnp.int32))[:, None]
    lag_row = jnp.arange(lag_count, dtype=jnp.int32)[None, :] - lag_count // 2
    phase_int = bins_col * lag_row % period
    angles = phase_int.astype(jnp.float32) * (2.0 * math.pi / period)
    return (jnp.cos(angles).astype(jnp.bfloat16), jnp.sin(angles).astype(jnp.bfloat16))

def reference(spectra, valid, sources, bounds):
    source_white = whiten(spectra[:, :, :, sources], valid[:, sources]).astype(jnp.float32)
    source_valid = valid[:, sources].astype(jnp.float32)
    cos_table, sin_table = make_tables(0, F, L, 2 * F)
    cos_f = cos_table.astype(jnp.float32)
    sin_f = sin_table.astype(jnp.float32)
    blocks = S // SRC_DEV

    def one_block(block_id):
        first = (block_id * CH_DEV).astype(jnp.int32)
        white_block = whiten(lax.dynamic_slice_in_dim(spectra, first, CH_DEV, 3), lax.dynamic_slice_in_dim(valid, first, CH_DEV, 1)).astype(jnp.float32)
        valid_block = lax.dynamic_slice_in_dim(valid, first, CH_DEV, 1).astype(jnp.float32)
        bound_block = lax.dynamic_slice_in_dim(bounds, first, CH_DEV, 1)
        cross_re = jnp.einsum('fws,fwc->fsc', source_white[0], white_block[0]) + jnp.einsum('fws,fwc->fsc', source_white[1], white_block[1])
        cross_im = jnp.einsum('fws,fwc->fsc', source_white[0], white_block[1]) - jnp.einsum('fws,fwc->fsc', source_white[1], white_block[0])
        pair_count = jnp.dot(source_valid.T, valid_block, preferred_element_type=jnp.float32)
        stack_re = (cross_re / pair_count).astype(jnp.bfloat16).astype(jnp.float32)
        stack_im = (cross_im / pair_count).astype(jnp.bfloat16).astype(jnp.float32)
        lag_corr = (jnp.einsum('fsc,ft->sct', stack_re, cos_f) - jnp.einsum('fsc,ft->sct', stack_im, sin_f)).astype(jnp.bfloat16)
        lag_index = jnp.arange(L, dtype=jnp.int32)[None, None, :]
        inside = (lag_index >= bound_block[:, :, 0:1]) & (lag_index < bound_block[:, :, 1:2])
        peak_value = lax.optimization_barrier(jnp.max(jnp.where(inside, lag_corr.astype(jnp.float32), -jnp.inf), axis=2))
        return (lag_corr, peak_value)
    corr_blocks, peak_blocks = lax.map(one_block, jnp.arange(blocks, dtype=jnp.int32))
    lag_corr = jnp.moveaxis(corr_blocks, 0, 1).reshape(S, C, L)
    peak_value = jnp.moveaxis(peak_blocks, 0, 1).reshape(S, C)
    return (lag_corr, peak_value)
```

```python
import math

import jax
import jax.numpy as jnp
from jax import lax
from jax.experimental import pallas as pl
from jax.experimental.pallas import tpu as pltpu
from jax.sharding import Mesh, PartitionSpec as P

F = 128
F2 = F // 2
L = 128
W = 384
WB = 96
CH = 128
K2 = 4 * WB
NS = 16
MB = 1 << 20
BF = jnp.bfloat16
F32 = jnp.float32
NT = (((1,), (1,)), ((), ()))


def shift(x, axis, step, size):
    return lax.ppermute(x, axis, [(k, (k + step) % size) for k in range(size)])


def pick_kernel(onehot_ref, spec_ref, valid_ref, out_ref, raw_ref, acc_ref):
    step = pl.program_id(0)
    onehot = onehot_ref[...]

    @pl.when(step == 0)
    def _():
        acc_ref[...] = jnp.zeros_like(acc_ref)

    acc = acc_ref[...]
    for k in range(8):
        cols = []
        for f in (2 * k, 2 * k + 1):
            for p in range(2):
                cols.append(spec_ref[p, f])
        rows = jnp.concatenate(cols, axis=0)
        raw = lax.dot_general(onehot, rows, NT, preferred_element_type=F32)
        raw_ref[step * 8 + k] = raw
        acc = acc + raw * raw
    acc_ref[...] = acc

    @pl.when(step == 7)
    def _():
        total = acc[:, 0:WB] + acc[:, WB:2 * WB] + acc[:, 2 * WB:3 * WB] + acc[:, 3 * WB:]
        picked_all = lax.dot_general(onehot, valid_ref[0], NT, preferred_element_type=F32)
        picked_own = lax.dot_general(onehot, valid_ref[1, :WB], NT, preferred_element_type=F32)
        scale = picked_own / jnp.sqrt(total * (1.0 / F) + 1e-6)
        scale4 = jnp.concatenate([scale] * 4, axis=1)

        @pl.loop(0, F2)
        def _(k):
            out_ref[k] = (raw_ref[k] * scale4)[:4].astype(BF)

        out_ref[F2] = picked_all[:4].astype(BF)


def pick(onehot, spectra, valid2):
    return pl.pallas_call(
        pick_kernel,
        grid=(8,),
        in_specs=[
            pl.BlockSpec((8, CH), lambda i: (0, 0)),
            pl.BlockSpec((2, 16, WB, CH), lambda i: (0, i, 0, 0)),
            pl.BlockSpec((2, W, CH), lambda i: (0, 0, 0)),
        ],
        out_specs=pl.BlockSpec((F2 + 1, 4, K2), lambda i: (0, 0, 0)),
        out_shape=jax.ShapeDtypeStruct((F2 + 1, 4, K2), BF),
        scratch_shapes=[pltpu.VMEM((F2, 8, K2), F32), pltpu.VMEM((8, K2), F32)],
        compiler_params=pltpu.CompilerParams(vmem_limit_bytes=40 * MB),
        cost_estimate=pl.CostEstimate(flops=2 * 10 ** 9, bytes_accessed=7 * 10 ** 6, transcendentals=0),
        name="pick_sources",
    )(onehot, spectra, valid2)


def whiten_kernel(spec_ref, valid_ref, out_ref):
    energy = jnp.zeros((16, CH), F32)
    for f in range(F):
        re = spec_ref[0, f].astype(F32)
        im = spec_ref[1, f].astype(F32)
        energy = energy + (re * re + im * im)
    scale = valid_ref[...].astype(F32) / jnp.sqrt(energy * (1.0 / F) + 1e-6)
    for f in range(F):
        for p in range(2):
            out_ref[p, f] = (spec_ref[p, f].astype(F32) * scale).astype(BF)


def whiten(spectra, own_valid):
    return pl.pallas_call(
        whiten_kernel,
        grid=(WB // 16,),
        in_specs=[
            pl.BlockSpec((2, F, 16, CH), lambda i: (0, 0, i, 0)),
            pl.BlockSpec((16, CH), lambda i: (i, 0)),
        ],
        out_specs=pl.BlockSpec((2, F, 16, CH), lambda i: (0, 0, i, 0)),
        out_shape=jax.ShapeDtypeStruct((2, F, WB, CH), BF),
        compiler_params=pltpu.CompilerParams(vmem_limit_bytes=40 * MB),
        cost_estimate=pl.CostEstimate(flops=10 ** 7, bytes_accessed=13 * 10 ** 6, transcendentals=0),
        name="whiten_channels",
    )(spectra, own_valid)


def cross_kernel(a_ref, b_ref, va_ref, vb_ref, chan_ref, valid_ref, table_ref,
                 out_a, out_b, cnt_a, cnt_b, x_ref):
    step = pl.program_id(0)
    n = 2 * NS
    pad = jnp.zeros((256 - 2 * WB, 2 * CH), BF)
    for k in range(8):
        lhs = jnp.concatenate([a_ref[k], b_ref[k]], axis=0)
        for odd in range(2):
            re = chan_ref[0, 2 * k + odd]
            im = chan_ref[1, 2 * k + odd]
            top = jnp.concatenate([re, im], axis=1)
            low = jnp.concatenate([im, -re], axis=1)
            if odd:
                rhs = jnp.concatenate([pad, top, low], axis=0)
                part = lhs[:, 128:]
            else:
                rhs = jnp.concatenate([top, low, pad], axis=0)
                part = lhs[:, :256]
            cross = jnp.dot(part, rhs, preferred_element_type=F32)
            f = step * 16 + 2 * k + odd
            x_ref[pl.ds(f, n, stride=2 * F), :] = cross[:, :CH]
            x_ref[pl.ds(F + f, n, stride=2 * F), :] = cross[:, CH:]

    @pl.when(step == 7)
    def _():
        valid = valid_ref[...]
        cnt_a[...] = jnp.dot(va_ref[0], valid, preferred_element_type=F32)
        cnt_b[...] = jnp.dot(vb_ref[0], valid, preferred_element_type=F32)
        table = table_ref[...]
        for out_ref, base in ((out_a, 0), (out_b, NS)):
            for s in range(0, NS, 2):
                first = x_ref[pl.ds((base + s) * 2 * F, 2 * F), :].astype(BF)
                second = x_ref[pl.ds((base + s + 1) * 2 * F, 2 * F), :].astype(BF)
                lag = jnp.dot(table, jnp.concatenate([first, second], axis=1), preferred_element_type=F32)
                out_ref[s] = lag[:, :CH].astype(BF)
                out_ref[s + 1] = lag[:, CH:].astype(BF)


def cross(a, b, chan, valid, table):
    part = pl.BlockSpec((8, NS, K2), lambda i: (i, 0, 0))
    tail = pl.BlockSpec((1, NS, K2), lambda i: (F2, 0, 0))
    out = pl.BlockSpec((NS, L, CH), lambda i: (0, 0, 0))
    cnt = pl.BlockSpec((NS, CH), lambda i: (0, 0))
    return pl.pallas_call(
        cross_kernel,
        grid=(8,),
        in_specs=[
            part, part, tail, tail,
            pl.BlockSpec((2, 16, WB, CH), lambda i: (0, i, 0, 0)),
            pl.BlockSpec((W, CH), lambda i: (0, 0)),
            pl.BlockSpec((L, 2 * F), lambda i: (0, 0)),
        ],
        out_specs=[out, out, cnt, cnt],
        out_shape=[jax.ShapeDtypeStruct((NS, L, CH), BF)] * 2 + [jax.ShapeDtypeStruct((NS, CH), F32)] * 2,
        scratch_shapes=[pltpu.VMEM((2 * NS * 2 * F, CH), F32)],
        compiler_params=pltpu.CompilerParams(vmem_limit_bytes=40 * MB),
        cost_estimate=pl.CostEstimate(flops=6 * 10 ** 9, bytes_accessed=10 * 10 ** 6, transcendentals=0),
        name="cross_lag",
    )(a, b, a, b, chan, valid, table)


def finish_kernel(rows_ref, bounds_ref, *refs):
    n_in = len(refs) - 2
    lag_ref, peak_ref = refs[n_in], refs[n_in + 1]
    lag_index = lax.broadcasted_iota(jnp.int32, (L, CH), 0)
    slot = 0
    for g in range(n_in // 3):
        keep_ref, recv_ref, cnt_ref = refs[3 * g], refs[3 * g + 1], refs[3 * g + 2]
        for r in range(recv_ref.shape[0]):
            row = rows_ref[slot]
            slot += 1
            total = keep_ref[r].astype(F32) + recv_ref[r].astype(F32)
            value = (total / cnt_ref[r:r + 1, :]).astype(BF)
            lag_ref[row] = value.T
            lower = bounds_ref[0, pl.ds(row, 1), :]
            upper = bounds_ref[1, pl.ds(row, 1), :]
            inside = (lag_index >= lower) & (lag_index < upper)
            best = jnp.max(jnp.where(inside, value.astype(F32), -jnp.inf), axis=0, keepdims=True)
            peak_ref[pl.ds(row, 1), :] = best


def finish(rows, bounds2, groups):
    flat = [x for g in groups for x in g]
    vm = pl.BlockSpec(memory_space=pltpu.VMEM)
    return pl.pallas_call(
        finish_kernel,
        in_specs=[pl.BlockSpec(memory_space=pltpu.SMEM)] + [vm] * (1 + len(flat)),
        out_specs=[vm, vm],
        out_shape=[jax.ShapeDtypeStruct((64, CH, L), BF), jax.ShapeDtypeStruct((64, CH), F32)],
        compiler_params=pltpu.CompilerParams(vmem_limit_bytes=50 * MB),
        cost_estimate=pl.CostEstimate(flops=10 ** 7, bytes_accessed=8 * 10 ** 6, transcendentals=0),
        name="finish_lags",
    )(rows, bounds2, *flat)


def lag_table():
    bins_col = (1 + jnp.arange(F, dtype=jnp.int32))[:, None]
    lag_row = jnp.arange(L, dtype=jnp.int32)[None, :] - L // 2
    angles = (bins_col * lag_row % (2 * F)).astype(F32) * (2.0 * math.pi / (2 * F))
    cos, sin = jnp.cos(angles).astype(BF), jnp.sin(angles).astype(BF)
    return jnp.concatenate([cos, -sin], axis=0).T


def add(a, b):
    return (a.astype(F32) + b.astype(F32)).astype(BF)


def local(spectra, valid, sources, bounds):
    xlo = lax.axis_index("xlo")
    core = lax.axis_index("core")
    y = lax.axis_index("y")
    xh = lax.axis_index("xh")
    z = lax.axis_index("z")
    freq = xlo * 2 + core
    offsets = sources - ((y * 2 + xh) * 8 + z) * CH
    offsets = jnp.concatenate([offsets, jnp.full((4,), -1, jnp.int32)])
    onehot = (offsets[:, None] == jnp.arange(CH, dtype=jnp.int32)[None, :]).astype(BF)
    valid_b = valid.astype(BF)
    own_valid = lax.dynamic_slice_in_dim(valid_b, freq * WB, WB, 0)
    valid2 = jnp.stack([valid_b, jnp.pad(own_valid, ((0, W - WB), (0, 0)))])
    table = lag_table()

    picked = pick(onehot, spectra, valid2)
    other = shift(picked, "xh", 1, 2)
    mine1 = jnp.concatenate([picked[:, :2], other[:, :2]], axis=1)
    mine2 = jnp.concatenate([picked[:, 2:], other[:, 2:]], axis=1)

    up = shift(mine1, "y", -1, 4)
    down = shift(mine1, "y", 1, 4)
    far = shift(mine1, "y", 2, 4)
    by_y = jnp.stack([mine1, up, far, down])
    order = [lax.dynamic_index_in_dim(by_y, ((freq ^ m) - y) % 4, 0, keepdims=False) for m in (0, 2, 1, 3)]
    ring = {0: jnp.concatenate(order, axis=1)}
    small = {0: mine2}
    for k in (1, 2, 3):
        small[-k] = shift(small[-(k - 1)], "z", 1, 8)
        small[k] = shift(small[k - 1], "z", -1, 8)
    small[4] = shift(small[3], "z", -1, 8)
    halves = ((0, 1, -1, 2), (-2, 3, -3, 4))
    side = []
    for h in halves:
        own = jnp.concatenate([small[k] for k in h], axis=1)
        side.append({0: own})
    cut = F2 // 2
    for s in side:
        s[-1] = shift(s[0], "y", 1, 4)
        s[1] = shift(s[0], "y", -1, 4)
        s[2] = jnp.concatenate([shift(s[-1][:cut], "y", 1, 4), shift(s[1][cut:], "y", -1, 4)], axis=0)
    for k in (1, 2, 3):
        ring[-k] = shift(ring[-(k - 1)], "z", 1, 8)
        ring[k] = shift(ring[k - 1], "z", -1, 8)
    ring[4] = jnp.concatenate([shift(ring[-3][:cut], "z", 1, 8), shift(ring[3][cut:], "z", -1, 8)], axis=0)

    chan = whiten(spectra, own_valid)

    def run(a, b):
        oa, ob, ca, cb = cross(a, b, chan, valid_b, table)
        return (oa, ca), (ob, cb)

    lag1, lag2 = {}, [{}, {}]
    lag1[0], lag2[0][0] = run(ring[0], side[0][0])
    lag1[1], lag1[-1] = run(ring[1], ring[-1])
    lag2[0][1], lag2[0][-1] = run(side[0][1], side[0][-1])
    lag1[2], lag1[-2] = run(ring[2], ring[-2])
    lag2[0][2], lag2[1][0] = run(side[0][2], side[1][0])
    lag2[1][1], lag2[1][-1] = run(side[1][1], side[1][-1])
    lag1[3], lag1[-3] = run(ring[3], ring[-3])
    lag1[4], lag2[1][2] = run(ring[4], side[1][2])

    groups, rows = [], []
    for k in (0, 1, -1, 2, -2, 3, -3, 4):
        lag, cnt = lag1[k]
        total = add(lag[:8], shift(lag[8:], "core", 1, 2))
        recv = shift(total[4:], "xlo", 1, 2)
        groups.append((total[:4], recv, cnt[:4]))
        for e in range(2):
            for j in range(2):
                rows.append((xh ^ e) * 32 + ((z + k) % 8) * 4 + j)
    even = (y % 2) == core
    for h in range(2):
        o = lag2[h]
        keep = (jnp.where(even, o[0][0], o[1][0]), jnp.where(even, o[2][0], o[-1][0]))
        send = (jnp.where(even, o[1][0], o[0][0]), jnp.where(even, o[-1][0], o[2][0]))
        t0 = add(keep[0], shift(send[0], "core", 1, 2))
        t1 = add(keep[1], shift(send[1], "core", 1, 2))
        first = jnp.where(even, y, (y + 1) % 4) == freq
        mine = jnp.where(first, t0, t1)
        away = jnp.where(first, t1, t0)
        recv = shift(away, "xlo", 1, 2)
        r = (freq - y) % 4
        cnt = lax.dynamic_index_in_dim(jnp.stack([o[0][1], o[1][1], o[2][1], o[-1][1]]), r, 0, keepdims=False)
        groups.append((mine, recv, cnt))
        for k in halves[h]:
            for e in range(2):
                for j in range(2):
                    rows.append((xh ^ e) * 32 + ((z + k) % 8) * 4 + 2 + j)
    rows = jnp.stack(rows).astype(jnp.int32)
    bounds2 = jnp.stack([bounds[:, :, 0], bounds[:, :, 1]])
    lag_corr, peak = finish(rows, bounds2, groups)
    return (lag_corr, peak)


def solution(mesh):
    fine = Mesh(mesh.devices.reshape(2, 2, 4, 2, 8), ("xlo", "core", "y", "xh", "z"))
    freq, rcv = ("xlo", "core"), ("y", "xh", "z")
    in_specs = (P(None, None, freq, rcv), P(None, rcv), P(rcv), P(freq, rcv, None))
    out_specs = (P(freq, rcv, None), P(freq, rcv))
    return jax.shard_map(local, mesh=fine, in_specs=in_specs, out_specs=out_specs, check_vma=False)
```

```python
import functools
import math

import jax
import jax.numpy as jnp
import numpy as np
from jax import lax
from jax.experimental import pallas as pl
from jax.experimental.pallas import tpu as pltpu
from jax.sharding import Mesh, PartitionSpec as P

F = 128
F2 = F // 2
L = 128
W = 384
WB = 96
CH = 128
K2 = 4 * WB
NS = 16
MB = 1 << 20
COST = 10 ** 6
BF = jnp.bfloat16
F32 = jnp.float32
NT = (((1,), (1,)), ((), ()))


def shift(x, axis, step, size):
    return lax.ppermute(x, axis, [(k, (k + step) % size) for k in range(size)])


def pick_kernel(place_ref, spec_hbm, valid_ref, out_ref, spec_ref, raw_ref, sems):
    def fetch(g):
        bins = pl.ds(g * 16, 16)
        return pltpu.make_async_copy(spec_hbm.at[:, bins], spec_ref.at[:, bins], sems.at[g])

    for g in range(8):
        fetch(g).start()
    lane = lax.broadcasted_iota(jnp.int32, (8, CH), 1)
    row = lax.broadcasted_iota(jnp.int32, (8, CH), 0)
    hit = jnp.zeros((8, CH), F32)
    for k in range(4):
        hit = jnp.where((row == k) & (lane == place_ref[k]), 1.0, hit)
    onehot = hit.astype(BF)
    own_first = pl.multiple_of(place_ref[4] * WB, 8)
    acc = jnp.zeros((8, K2), F32)
    for g in range(8):
        fetch(g).wait()
        for k in range(8 * g, 8 * g + 8):
            rows = jnp.concatenate([spec_ref[p, f] for f in (2 * k, 2 * k + 1) for p in range(2)], axis=0)
            raw = lax.dot_general(onehot, rows, NT, preferred_element_type=F32)
            raw_ref[k] = raw
            acc = acc + raw * raw
    total = acc[:, 0:WB] + acc[:, WB:2 * WB] + acc[:, 2 * WB:3 * WB] + acc[:, 3 * WB:]
    picked_all = lax.dot_general(onehot, valid_ref[...].astype(BF), NT, preferred_element_type=F32)
    picked_own = lax.dot_general(onehot, valid_ref[pl.ds(own_first, WB), :].astype(BF), NT, preferred_element_type=F32)
    scale = picked_own / jnp.sqrt(total * (1.0 / F) + 1e-6)
    scale4 = jnp.concatenate([scale] * 4, axis=1)

    @pl.loop(0, F2)
    def _(k):
        out_ref[k] = (raw_ref[k] * scale4)[:4].astype(BF)

    out_ref[F2] = picked_all[:4].astype(BF)


VM = pl.BlockSpec(memory_space=pltpu.VMEM)


def pick(place, spectra, valid):
    return pl.pallas_call(
        pick_kernel,
        in_specs=[pl.BlockSpec(memory_space=pltpu.SMEM), pl.BlockSpec(memory_space=pltpu.HBM), VM],
        out_specs=VM,
        out_shape=jax.ShapeDtypeStruct((F2 + 1, 4, K2), BF),
        scratch_shapes=[pltpu.VMEM((2, F, WB, CH), BF), pltpu.VMEM((F2, 8, K2), F32), pltpu.SemaphoreType.DMA((8,))],
        compiler_params=pltpu.CompilerParams(vmem_limit_bytes=58 * MB),
        cost_estimate=pl.CostEstimate(flops=2 * 10 ** 9, bytes_accessed=7 * 10 ** 6, transcendentals=0),
        name="pick_sources",
    )(place, spectra, valid)


def whiten_kernel(spec_ref, valid_ref, out_ref):
    @pl.loop(0, WB // 16)
    def _(g):
        rows = pl.ds(pl.multiple_of(g * 16, 16), 16)
        energy = jnp.zeros((16, CH), F32)
        for f in range(F):
            re = spec_ref[0, f, rows].astype(F32)
            im = spec_ref[1, f, rows].astype(F32)
            energy = energy + (re * re + im * im)
        scale = valid_ref[rows].astype(F32) / jnp.sqrt(energy * (1.0 / F) + 1e-6)
        for f in range(F):
            for p in range(2):
                out_ref[p, f, rows] = (spec_ref[p, f, rows].astype(F32) * scale).astype(BF)


def whiten(spectra, own_valid):
    return pl.pallas_call(
        whiten_kernel,
        in_specs=[VM, VM],
        out_specs=VM,
        out_shape=pltpu.VMEM((2, F, WB, CH), BF),
        compiler_params=pltpu.CompilerParams(vmem_limit_bytes=16 * MB),
        cost_estimate=pl.CostEstimate(flops=10 ** 6, bytes_accessed=10 ** 5, transcendentals=0),
        name="whiten_channels",
    )(spectra, own_valid)


def cross_kernel(n_ring, n_side, *refs):
    n_chunks = n_ring + n_side
    parts = refs[:n_chunks]
    valids = refs[n_chunks:2 * n_chunks]
    chan_ref, valid_ref, table_ref, keep_ref, send_ref, raw_ref, cnt_ref, x_ref = refs[2 * n_chunks:]
    step = pl.program_id(0)
    n = n_chunks * NS
    pad = jnp.zeros((256 - 2 * WB, 2 * CH), BF)
    held = []
    for k in range(8):
        lhs = jnp.concatenate([part[k] for part in parts], axis=0)
        for odd in range(2):
            re = chan_ref[0, step * 16 + 2 * k + odd]
            im = chan_ref[1, step * 16 + 2 * k + odd]
            top = jnp.concatenate([re, im], axis=1)
            low = jnp.concatenate([im, -re], axis=1)
            if odd:
                rhs = jnp.concatenate([pad, top, low], axis=0)
                used = lhs[:, 128:]
            else:
                rhs = jnp.concatenate([top, low, pad], axis=0)
                used = lhs[:, :256]
            both = jnp.dot(used, rhs, preferred_element_type=F32)
            held.append(both.astype(BF))
    for p in range(2):
        block = jnp.stack([h[:, p * CH:(p + 1) * CH] for h in held])
        first_bin = pl.multiple_of(p * F + step * 16, 16)
        x_ref[:, pl.ds(first_bin, 16), :] = jnp.transpose(block, (1, 0, 2))

    @pl.when(step == 7)
    def _():
        for c in range(n_chunks):
            cnt_ref[c * NS:(c + 1) * NS] = jnp.dot(valids[c][0], valid_ref[...], preferred_element_type=F32)
        table = table_ref[...]

        def pair(out_ref, slot, row):
            lag = jnp.dot(table, jnp.concatenate([x_ref[row], x_ref[row + 1]], axis=1), preferred_element_type=F32)
            out_ref[slot] = lag[:, :CH].astype(BF)
            out_ref[slot + 1] = lag[:, CH:].astype(BF)

        for block, (out_ref, half) in enumerate(((keep_ref, 0), (keep_ref, 1), (send_ref, 0), (send_ref, 1))):
            for c in range(n_ring):
                for q in range(0, NS // 4, 2):
                    pair(out_ref, half * (n_ring * 4) + c * 4 + q, c * NS + block * 4 + q)
        for q in range(0, n_side * NS, 2):
            pair(raw_ref, q, n_ring * NS + q)


def cross(ring, side, chan, valid, table):
    chunks = list(ring) + list(side)
    n_ring, n_side, n_chunks = len(ring), len(side), len(chunks)
    n = n_chunks * NS
    part = pl.BlockSpec((8, NS, K2), lambda i: (i, 0, 0))
    tail = pl.BlockSpec((1, NS, K2), lambda i: (F2, 0, 0))
    sizes = [max(n_ring * 8, 1)] * 2 + [max(n_side * NS, 1)]
    return pl.pallas_call(
        functools.partial(cross_kernel, n_ring, n_side),
        grid=(8,),
        in_specs=[part] * n_chunks + [tail] * n_chunks + [
            VM,
            pl.BlockSpec((W, CH), lambda i: (0, 0)),
            pl.BlockSpec((L, 2 * F), lambda i: (0, 0)),
        ],
        out_specs=[pl.BlockSpec((k, L, CH), lambda i: (0, 0, 0)) for k in sizes] + [pl.BlockSpec((n, CH), lambda i: (0, 0))],
        out_shape=[jax.ShapeDtypeStruct((k, L, CH), BF) for k in sizes] + [jax.ShapeDtypeStruct((n, CH), F32)],
        scratch_shapes=[pltpu.VMEM((n, 2 * F, CH), BF)],
        compiler_params=pltpu.CompilerParams(vmem_limit_bytes=24 * MB),
        cost_estimate=pl.CostEstimate(flops=COST * n_chunks, bytes_accessed=10 ** 5 * n_chunks, transcendentals=0),
        name="cross_lag",
    )(*chunks, *chunks, chan, valid, table)


def finish_kernel(rows_ref, live_ref, bounds_ref, *refs):
    n_in = len(refs) - 2
    lag_ref, peak_ref = refs[n_in], refs[n_in + 1]
    lag_index = lax.broadcasted_iota(jnp.int32, (L, CH), 0)
    first = 0
    for g in range(n_in // 3):
        keep_ref, recv_ref, cnt_ref = refs[3 * g], refs[3 * g + 1], refs[3 * g + 2]
        count = recv_ref.shape[0]

        def one(r, keep_ref=keep_ref, recv_ref=recv_ref, cnt_ref=cnt_ref, first=first):
            row = rows_ref[first + r]
            total = keep_ref[r].astype(F32) + recv_ref[r].astype(F32)
            value = (total / cnt_ref[pl.ds(r, 1), :]).astype(BF)
            lag_ref[row] = value.T
            lower = bounds_ref[0, pl.ds(row, 1), :]
            upper = bounds_ref[1, pl.ds(row, 1), :]
            inside = (lag_index >= lower) & (lag_index < upper)
            best = jnp.max(jnp.where(inside, value.astype(F32), -jnp.inf), axis=0, keepdims=True)
            peak_ref[pl.ds(row, 1), :] = best

        @pl.when(live_ref[g] != 0)
        def _(one=one, count=count):
            @pl.loop(0, count // 4)
            def _(q):
                for k in range(4):
                    one(q * 4 + k)
        first += count


def finish(rows, live, bounds2, groups):
    flat = [x for g in groups for x in g]
    smem = pl.BlockSpec(memory_space=pltpu.SMEM)
    return pl.pallas_call(
        finish_kernel,
        in_specs=[smem, smem] + [VM] * (1 + len(flat)),
        out_specs=[VM, VM],
        out_shape=[jax.ShapeDtypeStruct((64, CH, L), BF), jax.ShapeDtypeStruct((64, CH), F32)],
        compiler_params=pltpu.CompilerParams(vmem_limit_bytes=24 * MB),
        cost_estimate=pl.CostEstimate(flops=10 ** 7, bytes_accessed=8 * 10 ** 6, transcendentals=0),
        name="finish_lags",
    )(rows, live, bounds2, *flat)


def lag_table():
    bins_col = (1 + jnp.arange(F, dtype=jnp.int32))[:, None]
    lag_row = jnp.arange(L, dtype=jnp.int32)[None, :] - L // 2
    angles = (bins_col * lag_row % (2 * F)).astype(F32) * (2.0 * math.pi / (2 * F))
    cos, sin = jnp.cos(angles).astype(BF), jnp.sin(angles).astype(BF)
    return jnp.concatenate([cos, -sin], axis=0).T


def tie(values):
    return lax.optimization_barrier(values)


def add(a, b):
    return (a.astype(F32) + b.astype(F32)).astype(BF)


def local(spectra, valid, sources, bounds):
    xlo = lax.axis_index("xlo")
    core = lax.axis_index("core")
    y = lax.axis_index("y")
    xh = lax.axis_index("xh")
    z = lax.axis_index("z")
    freq = xlo * 2 + core
    offsets = sources - ((y * 2 + xh) * 8 + z) * CH
    place = jnp.concatenate([offsets, freq[None].astype(jnp.int32)])
    valid_b = valid.astype(BF)
    own_valid = lax.dynamic_slice_in_dim(valid_b, freq * WB, WB, 0)
    table = lag_table()

    picked = pick(place, spectra, valid)
    other = shift(picked, "xh", 1, 2)
    mine1 = jnp.concatenate([picked[:, :2], other[:, :2]], axis=1)
    mine2 = jnp.concatenate([picked[:, 2:], other[:, 2:]], axis=1)

    def swap_core(part):
        keep, send, cnt = part
        got = shift(send, "core", 1, 2)
        half = keep.shape[0] // 2
        return add(keep[:half], got[:half]), add(keep[half:], got[half:]), cnt

    def swap_x(part):
        mine, away, cnt = part
        return mine, shift(away, "xlo", 1, 2), cnt

    def side_core(lags, odd):
        pairs = [((1 - c) * 4 + k, c * 4 + k) for k in range(4) for c in range(2) if c == (k + odd) % 2]
        return add(lags, lax.ppermute(lags, ("core", "y"), pairs))

    def side_x(total, odd, low_is_mine):
        half = total.shape[0] // 2
        pairs = [((h * 2 + c) * 4 + k, ((1 - h) * 2 + c) * 4 + k)
                 for k in range(4) for c in range(2) for h in range(2) if c == (k + odd) % 2]
        mine = jnp.where(low_is_mine, total[:half], total[half:])
        away = jnp.where(low_is_mine, total[half:], total[:half])
        return mine, lax.ppermute(away, ("xlo", "core", "y"), pairs)

    r = (freq - y) % 4
    halves = ((0, 1, -1, 2), (-2, 3, -3, 4))

    def lanes(ks, first):
        return [(k, e, first + j) for k in ks for e in range(2) for j in range(2)]

    spots = []
    for ks in ((0,), (1, -1), (2, -2), (3, -3), (4,)):
        spots += lanes(ks, 0)
    spots += lanes(halves[0], 2) + lanes(halves[1], 2)
    one = spots + lanes(halves[0], 2) + lanes(halves[1], 2)
    two = spots + lanes(halves[1], 2) + lanes(halves[0], 2)
    tables = np.array([one, two], np.int32)
    spot = jnp.where(r == 1, tables[0], tables[1])
    rows = ((xh ^ spot[:, 1]) * 32 + ((z + spot[:, 0]) % 8) * 4 + spot[:, 2]).astype(jnp.int32)
    even = 1 - r % 2
    live = jnp.where(np.arange(8) < 5, 1, jnp.where(np.arange(8) == 5, even, 1 - even)).astype(jnp.int32)
    bounds2 = jnp.stack([bounds[:, :, 0], bounds[:, :, 1]])

    r1 = (shift(mine1, "y", -1, 4), shift(mine1, "y", 2, 4), shift(mine1, "y", 1, 4))
    b1, bm1 = shift(mine2, "z", -1, 8), shift(mine2, "z", 1, 8)
    b2, bm2 = shift(b1, "z", -1, 8), shift(bm1, "z", 1, 8)
    b3, bm3 = shift(b2, "z", -1, 8), shift(bm2, "z", 1, 8)
    up, far, down = r1
    by_y = jnp.stack([mine1, up, far, down])
    order = [lax.dynamic_index_in_dim(by_y, ((freq ^ m) - y) % 4, 0, keepdims=False) for m in (0, 2, 1, 3)]
    a0 = jnp.concatenate(order, axis=1)
    h0 = [jnp.concatenate([mine2, b1, bm1, b2], axis=1)]
    a0, h0, bm2, b3, bm3, rows, live = tie((a0, h0, bm2, b3, bm3, rows, live))
    chan = whiten(spectra, own_valid)

    def run(ring, side=()):
        return cross(ring, side, chan, valid_b, table)

    a1, am1 = shift(a0, "z", -1, 8), shift(a0, "z", 1, 8)
    h0.append(shift(h0[0], "y", -1, 4))
    b4 = shift(b3, "z", -1, 8)
    h1 = [jnp.concatenate([bm2, b3, bm3, b4], axis=1)]
    h1.append(shift(h1[0], "y", 1, 4))
    kp, sd, _, cnt0 = run([a0])
    a1, am1, h0, h1, kp, sd = tie((a1, am1, h0, h1, kp, sd))
    a2, am2 = shift(a1, "z", -1, 8), shift(am1, "z", 1, 8)
    h0.append(shift(h0[1], "y", -1, 4))
    h1.append(shift(h1[1], "y", 1, 4))
    k0 = swap_core((kp, sd, cnt0))
    kp, sd, raw1, cnt1 = run([a1, am1], [h0[1], h1[1]])
    a2, am2, h0, h1, k0, kp, sd, raw1 = tie((a2, am2, h0, h1, k0, kp, sd, raw1))
    a3, am3 = shift(a2, "z", -1, 8), shift(am2, "z", 1, 8)
    h0.append(shift(h0[2], "y", -1, 4))
    h1.append(shift(h1[2], "y", 1, 4))
    k0 = swap_x(k0)
    k1 = swap_core((kp, sd, cnt1))
    p1 = side_core(raw1, 1)
    _, _, raw0, cntp = run([], [h0[0], h1[0], h0[2], h1[2]])
    kp, sd, _, cnt2 = run([a2, am2])
    p0 = side_core(raw0, 0)
    a3, am3, h0, h1, k0, k1, p1, kp, sd, p0 = tie((a3, am3, h0, h1, k0, k1, p1, kp, sd, p0))
    cut = F2 // 2
    a4 = jnp.concatenate([shift(am3[:cut], "z", 1, 8), shift(a3[cut:], "z", -1, 8)], axis=0)
    p0 = side_x(p0, 0, r == 0)
    k1 = swap_x(k1)
    p1 = side_x(p1, 1, r == 1)
    k2 = swap_core((kp, sd, cnt2))
    kp, sd, raw3, cnt3 = run([a3, am3], [h0[3], h1[3]])
    a4, k2, kp, sd, raw3 = tie((a4, k2, kp, sd, raw3))
    k2 = swap_x(k2)
    p3 = side_x(side_core(raw3, 1), 1, r == 3)
    k3 = swap_x(swap_core((kp, sd, cnt3)))
    kp, sd, _, cnt4 = run([a4])
    k4 = swap_x(swap_core((kp, sd, cnt4)))

    groups = []
    for ks, (mine, recv, cnt) in ((1, k0), (2, k1), (2, k2), (2, k3), (1, k4)):
        groups.append((mine, recv, jnp.concatenate([cnt[c * NS:c * NS + 4] for c in range(ks)], axis=0)))
    groups.append((*p0, jnp.where(r == 0, cntp[:2 * NS], cntp[2 * NS:])))
    cnt1, cnt3 = cnt1[2 * NS:], cnt3[2 * NS:]
    groups.append((*p1, jnp.where(r == 1, cnt1[:NS], cnt1[NS:])))
    groups.append((*p3, jnp.where(r == 3, cnt3[:NS], cnt3[NS:])))
    lag_corr, peak = finish(rows, live, bounds2, groups)
    return (lag_corr, peak)


def solution(mesh):
    fine = Mesh(mesh.devices.reshape(2, 2, 4, 2, 8), ("xlo", "core", "y", "xh", "z"))
    freq, rcv = ("xlo", "core"), ("y", "xh", "z")
    in_specs = (P(None, None, freq, rcv), P(None, rcv), P(rcv), P(freq, rcv, None))
    out_specs = (P(freq, rcv, None), P(freq, rcv))
    return jax.shard_map(local, mesh=fine, in_specs=in_specs, out_specs=out_specs, check_vma=False)
```

```python
import functools
import math

import jax
import jax.numpy as jnp
import numpy as np
from jax import lax
from jax.experimental import pallas as pl
from jax.experimental.pallas import tpu as pltpu
from jax.sharding import Mesh, PartitionSpec as P

F = 128
F2 = F // 2
L = 128
W = 384
WB = 96
CH = 128
K2 = 4 * WB
NS = 16
MB = 1 << 20
COST = 10 ** 6
BF = jnp.bfloat16
F32 = jnp.float32
NT = (((1,), (1,)), ((), ()))


def shift(x, axis, step, size):
    return lax.ppermute(x, axis, [(k, (k + step) % size) for k in range(size)])


def pick_kernel(place_ref, spec_hbm, valid_ref, out_ref, spec_ref, raw_ref, sems):
    def fetch(g):
        bins = pl.ds(g * 16, 16)
        return pltpu.make_async_copy(spec_hbm.at[:, bins], spec_ref.at[:, bins], sems.at[g])

    for g in range(8):
        fetch(g).start()
    lane = lax.broadcasted_iota(jnp.int32, (8, CH), 1)
    row = lax.broadcasted_iota(jnp.int32, (8, CH), 0)
    hit = jnp.zeros((8, CH), F32)
    for k in range(4):
        hit = jnp.where((row == k) & (lane == place_ref[k]), 1.0, hit)
    onehot = hit.astype(BF)
    own_first = pl.multiple_of(place_ref[4] * WB, 8)

    def block(g, acc):
        fetch(g).wait()
        for j in range(8):
            k = 8 * g + j
            rows = jnp.concatenate([spec_ref[p, 2 * k + odd] for odd in range(2) for p in range(2)], axis=0)
            raw = lax.dot_general(onehot, rows, NT, preferred_element_type=F32)
            raw_ref[k] = raw
            acc = acc + raw * raw
        return acc

    acc = lax.fori_loop(0, 8, block, jnp.zeros((8, K2), F32))
    total = acc[:, 0:WB] + acc[:, WB:2 * WB] + acc[:, 2 * WB:3 * WB] + acc[:, 3 * WB:]
    picked_all = lax.dot_general(onehot, valid_ref[...].astype(BF), NT, preferred_element_type=F32)
    picked_own = lax.dot_general(onehot, valid_ref[pl.ds(own_first, WB), :].astype(BF), NT, preferred_element_type=F32)
    scale = picked_own / jnp.sqrt(total * (1.0 / F) + 1e-6)
    scale4 = jnp.concatenate([scale] * 4, axis=1)

    @pl.loop(0, F2)
    def _(k):
        out_ref[k] = (raw_ref[k] * scale4)[:4].astype(BF)

    out_ref[F2] = picked_all[:4].astype(BF)


VM = pl.BlockSpec(memory_space=pltpu.VMEM)


def pick(place, spectra, valid):
    return pl.pallas_call(
        pick_kernel,
        in_specs=[pl.BlockSpec(memory_space=pltpu.SMEM), pl.BlockSpec(memory_space=pltpu.HBM), VM],
        out_specs=VM,
        out_shape=jax.ShapeDtypeStruct((F2 + 1, 4, K2), BF),
        scratch_shapes=[pltpu.VMEM((2, F, WB, CH), BF), pltpu.VMEM((F2, 8, K2), F32), pltpu.SemaphoreType.DMA((8,))],
        compiler_params=pltpu.CompilerParams(vmem_limit_bytes=58 * MB),
        cost_estimate=pl.CostEstimate(flops=2 * 10 ** 9, bytes_accessed=7 * 10 ** 6, transcendentals=0),
        name="pick_sources",
    )(place, spectra, valid)


def whiten_kernel(spec_ref, valid_ref, out_ref):
    @pl.loop(0, WB // 16)
    def _(g):
        rows = pl.ds(pl.multiple_of(g * 16, 16), 16)

        def power(g, energy):
            for f in range(16):
                re = spec_ref[0, g * 16 + f, rows].astype(F32)
                im = spec_ref[1, g * 16 + f, rows].astype(F32)
                energy = energy + (re * re + im * im)
            return energy

        energy = lax.fori_loop(0, F // 16, power, jnp.zeros((16, CH), F32))
        scale = valid_ref[rows].astype(F32) / jnp.sqrt(energy * (1.0 / F) + 1e-6)

        @pl.loop(0, F // 16)
        def _(g):
            for f in range(16):
                for p in range(2):
                    out_ref[p, g * 16 + f, rows] = (spec_ref[p, g * 16 + f, rows].astype(F32) * scale).astype(BF)


def whiten(spectra, own_valid):
    return pl.pallas_call(
        whiten_kernel,
        in_specs=[VM, VM],
        out_specs=VM,
        out_shape=pltpu.VMEM((2, F, WB, CH), BF),
        compiler_params=pltpu.CompilerParams(vmem_limit_bytes=16 * MB),
        cost_estimate=pl.CostEstimate(flops=10 ** 6, bytes_accessed=10 ** 5, transcendentals=0),
        name="whiten_channels",
    )(spectra, own_valid)


def cross_kernel(n_ring, n_side, *refs):
    n_chunks = n_ring + n_side
    parts = refs[:n_chunks]
    valids = refs[n_chunks:2 * n_chunks]
    chan_ref, valid_ref, table_ref, keep_ref, send_ref, cnt_ref, x_ref = refs[2 * n_chunks:]
    step = pl.program_id(0)
    n = n_chunks * NS
    pad = jnp.zeros((256 - 2 * WB, 2 * CH), BF)
    held = []
    for k in range(8):
        lhs = jnp.concatenate([part[k] for part in parts], axis=0)
        for odd in range(2):
            re = chan_ref[0, step * 16 + 2 * k + odd]
            im = chan_ref[1, step * 16 + 2 * k + odd]
            top = jnp.concatenate([re, im], axis=1)
            low = jnp.concatenate([im, -re], axis=1)
            if odd:
                rhs = jnp.concatenate([pad, top, low], axis=0)
                used = lhs[:, 128:]
            else:
                rhs = jnp.concatenate([top, low, pad], axis=0)
                used = lhs[:, :256]
            both = jnp.dot(used, rhs, preferred_element_type=F32)
            held.append(both.astype(BF))
    for p in range(2):
        block = jnp.stack([h[:, p * CH:(p + 1) * CH] for h in held])
        first_bin = pl.multiple_of(p * F + step * 16, 16)
        x_ref[:, pl.ds(first_bin, 16), :] = jnp.transpose(block, (1, 0, 2))

    @pl.when(step == 7)
    def _():
        for c in range(n_chunks):
            cnt_ref[c * NS:(c + 1) * NS] = jnp.dot(valids[c][0], valid_ref[...], preferred_element_type=F32)
        table = table_ref[...]

        def pair(out_ref, slot, row):
            lag = jnp.dot(table, jnp.concatenate([x_ref[row], x_ref[row + 1]], axis=1), preferred_element_type=F32)
            out_ref[slot] = lag[:, :CH].astype(BF)
            out_ref[slot + 1] = lag[:, CH:].astype(BF)

        for block, (out_ref, half) in enumerate(((keep_ref, 0), (keep_ref, 1), (send_ref, 0), (send_ref, 1))):
            for c in range(n_ring):
                for q in range(0, NS // 4, 2):
                    pair(out_ref, half * (n_ring * 4) + c * 4 + q, c * NS + block * 4 + q)

        if n_side:
            for q in range(0, n_side * NS, 2):
                pair(send_ref, n_ring * 8 + q, n_ring * NS + q)


def cross(ring, side, chan, valid, table):
    chunks = list(ring) + list(side)
    n_ring, n_side, n_chunks = len(ring), len(side), len(chunks)
    n = n_chunks * NS
    part = pl.BlockSpec((8, NS, K2), lambda i: (i, 0, 0))
    tail = pl.BlockSpec((1, NS, K2), lambda i: (F2, 0, 0))
    sizes = [n_ring * 8, n_ring * 8 + n_side * NS]
    return pl.pallas_call(
        functools.partial(cross_kernel, n_ring, n_side),
        grid=(8,),
        in_specs=[part] * n_chunks + [tail] * n_chunks + [
            VM,
            pl.BlockSpec((W, CH), lambda i: (0, 0)),
            pl.BlockSpec((L, 2 * F), lambda i: (0, 0)),
        ],
        out_specs=[pl.BlockSpec((k, L, CH), lambda i: (0, 0, 0)) for k in sizes] + [pl.BlockSpec((n, CH), lambda i: (0, 0))],
        out_shape=[jax.ShapeDtypeStruct((k, L, CH), BF) for k in sizes] + [jax.ShapeDtypeStruct((n, CH), F32)],
        scratch_shapes=[pltpu.VMEM((n, 2 * F, CH), BF)],
        compiler_params=pltpu.CompilerParams(vmem_limit_bytes=24 * MB),
        cost_estimate=pl.CostEstimate(flops=COST * n_chunks, bytes_accessed=10 ** 5 * n_chunks, transcendentals=0),
        name="cross_lag",
    )(*chunks, *chunks, chan, valid, table)


def finish_kernel(rows_ref, live_ref, bounds_ref, *refs):
    n_in = len(refs) - 2
    lag_ref, peak_ref = refs[n_in], refs[n_in + 1]
    lag_index = lax.broadcasted_iota(jnp.int32, (L, CH), 0)
    first = 0
    for g in range(n_in // 3):
        keep_ref, recv_ref, cnt_ref = refs[3 * g], refs[3 * g + 1], refs[3 * g + 2]
        count = recv_ref.shape[0]

        def one(r, keep_ref=keep_ref, recv_ref=recv_ref, cnt_ref=cnt_ref, first=first):
            row = rows_ref[first + r]
            total = keep_ref[r].astype(F32) + recv_ref[r].astype(F32)
            value = (total / cnt_ref[pl.ds(r, 1), :]).astype(BF)
            lag_ref[row] = value.T
            lower = bounds_ref[0, pl.ds(row, 1), :]
            upper = bounds_ref[1, pl.ds(row, 1), :]
            inside = (lag_index >= lower) & (lag_index < upper)
            best = jnp.max(jnp.where(inside, value.astype(F32), -jnp.inf), axis=0, keepdims=True)
            peak_ref[pl.ds(row, 1), :] = best

        @pl.when(live_ref[g] != 0)
        def _(one=one, count=count):
            @pl.loop(0, count // 4)
            def _(q):
                for k in range(4):
                    one(q * 4 + k)
        first += count


def finish(rows, live, bounds2, groups):
    flat = [x for g in groups for x in g]
    smem = pl.BlockSpec(memory_space=pltpu.SMEM)
    return pl.pallas_call(
        finish_kernel,
        in_specs=[smem, smem] + [VM] * (1 + len(flat)),
        out_specs=[VM, VM],
        out_shape=[jax.ShapeDtypeStruct((64, CH, L), BF), jax.ShapeDtypeStruct((64, CH), F32)],
        compiler_params=pltpu.CompilerParams(vmem_limit_bytes=24 * MB),
        cost_estimate=pl.CostEstimate(flops=10 ** 7, bytes_accessed=8 * 10 ** 6, transcendentals=0),
        name="finish_lags",
    )(rows, live, bounds2, *flat)


def lag_table():
    bins_col = (1 + jnp.arange(F, dtype=jnp.int32))[:, None]
    lag_row = jnp.arange(L, dtype=jnp.int32)[None, :] - L // 2
    angles = (bins_col * lag_row % (2 * F)).astype(F32) * (2.0 * math.pi / (2 * F))
    cos, sin = jnp.cos(angles).astype(BF), jnp.sin(angles).astype(BF)
    return jnp.concatenate([cos, -sin], axis=0).T


def tie(values):
    return lax.optimization_barrier(values)


def add(a, b):
    return (a.astype(F32) + b.astype(F32)).astype(BF)


def local(spectra, valid, sources, bounds):
    xlo = lax.axis_index("xlo")
    core = lax.axis_index("core")
    y = lax.axis_index("y")
    xh = lax.axis_index("xh")
    z = lax.axis_index("z")
    freq = xlo * 2 + core
    offsets = sources - ((y * 2 + xh) * 8 + z) * CH
    place = jnp.concatenate([offsets, freq[None].astype(jnp.int32)])
    valid_b = valid.astype(BF)
    own_valid = lax.dynamic_slice_in_dim(valid_b, freq * WB, WB, 0)
    table = lag_table()

    picked = pick(place, spectra, valid)
    other = shift(picked, "xh", 1, 2)
    mine1 = jnp.concatenate([picked[:, :2], other[:, :2]], axis=1)
    mine2 = jnp.concatenate([picked[:, 2:], other[:, 2:]], axis=1)

    def swap_core(keep, send):
        got = shift(send, "core", 1, 2)
        n, half = keep.shape[0], keep.shape[0] // 2
        side = add(send[n:], got[n:]) if send.shape[0] > n else None
        return add(keep[:half], got[:half]), add(keep[half:], got[half:n]), side

    def swap_x(mine, away):
        return mine, shift(away, "xlo", 1, 2)

    def side_x(total, odd, low_is_mine):
        half = total.shape[0] // 2
        pairs = [((h * 2 + c) * 4 + k, ((1 - h) * 2 + c) * 4 + k)
                 for k in range(4) for c in range(2) for h in range(2) if c == (k + odd) % 2]
        mine = jnp.where(low_is_mine, total[:half], total[half:])
        away = jnp.where(low_is_mine, total[half:], total[:half])
        return mine, lax.ppermute(away, ("xlo", "core", "y"), pairs)

    r = (freq - y) % 4
    halves = ((0, 1, -1, 2), (-2, 3, -3, 4))

    def lanes(ks, first):
        return [(k, e, first + j) for k in ks for e in range(2) for j in range(2)]

    spots = []
    for ks in ((0, 1, -1), (2, -2), (3, -3), (4,)):
        spots += lanes(ks, 0)
    spots += lanes(halves[0], 2) + lanes(halves[1], 2)
    one = spots + lanes(halves[0], 2) + lanes(halves[1], 2)
    two = spots + lanes(halves[1], 2) + lanes(halves[0], 2)
    tables = np.array([one, two], np.int32)
    spot = jnp.where(r == 1, tables[0], tables[1])
    rows = ((xh ^ spot[:, 1]) * 32 + ((z + spot[:, 0]) % 8) * 4 + spot[:, 2]).astype(jnp.int32)
    even = 1 - r % 2
    live = jnp.where(np.arange(7) < 4, 1, jnp.where(np.arange(7) == 4, even, 1 - even)).astype(jnp.int32)
    bounds2 = jnp.stack([bounds[:, :, 0], bounds[:, :, 1]])

    r1 = (shift(mine1, "y", -1, 4), shift(mine1, "y", 2, 4), shift(mine1, "y", 1, 4))
    b1, bm1 = shift(mine2, "z", -1, 8), shift(mine2, "z", 1, 8)
    b2, bm2 = shift(b1, "z", -1, 8), shift(bm1, "z", 1, 8)
    b3, bm3 = shift(b2, "z", -1, 8), shift(bm2, "z", 1, 8)
    up, far, down = r1
    by_y = jnp.stack([mine1, up, far, down])
    order = [lax.dynamic_index_in_dim(by_y, ((freq ^ m) - y) % 4, 0, keepdims=False) for m in (0, 2, 1, 3)]
    a0 = jnp.concatenate(order, axis=1)
    h0 = [jnp.concatenate([mine2, b1, bm1, b2], axis=1)]
    a0, h0, bm2, b3, bm3, rows, live = tie((a0, h0, bm2, b3, bm3, rows, live))
    chan = whiten(spectra, own_valid)

    def run(ring, side=(), after=()):
        gated = tie((table,) + tuple(after))[0] if after else table
        return cross(ring, side, chan, valid_b, gated)

    a1, am1 = shift(a0, "z", -1, 8), shift(a0, "z", 1, 8)
    h0.append(shift(h0[0], "y", -1, 4))
    b4 = shift(b3, "z", -1, 8)
    h1 = [jnp.concatenate([bm2, b3, bm3, b4], axis=1)]
    h1.append(shift(h1[0], "y", 1, 4))
    a1, am1, h0, h1, chan = tie((a1, am1, h0, h1, chan))
    a2, am2 = shift(a1, "z", -1, 8), shift(am1, "z", 1, 8)
    h0.append(shift(h0[1], "y", -1, 4))
    h1.append(shift(h1[1], "y", 1, 4))
    keep1, send1, cnt1 = run([a0, a1, am1], [h0[1], h1[1]])
    a2, am2, h0, h1, keep1, send1 = tie((a2, am2, h0, h1, keep1, send1))
    a3, am3 = shift(a2, "z", -1, 8), shift(am2, "z", 1, 8)
    h0.append(shift(h0[2], "y", -1, 4))
    h1.append(shift(h1[2], "y", 1, 4))
    mine1, away1, side1 = swap_core(keep1, send1)
    keep2, send2, cnt2 = run([a2, am2], [h0[0], h1[0], h0[2], h1[2]], (side1,))
    k1 = swap_x(mine1, away1)
    a3, am3, h0, h1, k1, side1, keep2, send2 = tie((a3, am3, h0, h1, k1, side1, keep2, send2))
    cut = F2 // 2
    a4 = jnp.concatenate([shift(am3[:cut], "z", 1, 8), shift(a3[cut:], "z", -1, 8)], axis=0)
    p1 = side_x(side1, 1, r == 1)
    mine2, away2, side2 = swap_core(keep2, send2)
    keep3, send3, cnt3 = run([a3, am3], [h0[3], h1[3]])
    a4, p1, side2, mine2, away2, keep3, send3 = tie((a4, p1, side2, mine2, away2, keep3, send3))
    p0 = side_x(side2, 0, r == 0)
    k2 = swap_x(mine2, away2)
    mine3, away3, side3 = swap_core(keep3, send3)
    p3 = side_x(side3, 1, r == 3)
    k3 = swap_x(mine3, away3)
    keep4, send4, cnt4 = run([a4], (), (side3,))
    mine4, away4, _ = swap_core(keep4, send4)
    k4 = swap_x(mine4, away4)

    groups = []
    for ks, (mine, recv), cnt in ((3, k1, cnt1), (2, k2, cnt2), (2, k3, cnt3), (1, k4, cnt4)):
        groups.append((mine, recv, jnp.concatenate([cnt[c * NS:c * NS + 4] for c in range(ks)], axis=0)))
    cnt1, cnt2, cnt3 = cnt1[3 * NS:], cnt2[2 * NS:], cnt3[2 * NS:]
    groups.append((*p0, jnp.where(r == 0, cnt2[:2 * NS], cnt2[2 * NS:])))
    groups.append((*p1, jnp.where(r == 1, cnt1[:NS], cnt1[NS:])))
    groups.append((*p3, jnp.where(r == 3, cnt3[:NS], cnt3[NS:])))
    lag_corr, peak = finish(rows, live, bounds2, groups)
    return (lag_corr, peak)


def solution(mesh):
    fine = Mesh(mesh.devices.reshape(2, 2, 4, 2, 8), ("xlo", "core", "y", "xh", "z"))
    freq, rcv = ("xlo", "core"), ("y", "xh", "z")
    in_specs = (P(None, None, freq, rcv), P(None, rcv), P(rcv), P(freq, rcv, None))
    out_specs = (P(freq, rcv, None), P(freq, rcv))
    return jax.shard_map(local, mesh=fine, in_specs=in_specs, out_specs=out_specs, check_vma=False)
```

```python
import functools
import math

import jax
import jax.numpy as jnp
import numpy as np
from jax import lax
from jax.experimental import pallas as pl
from jax.experimental.pallas import tpu as pltpu
from jax.sharding import Mesh, PartitionSpec as P

F = 128
F2 = F // 2
L = 128
W = 384
WB = 96
CH = 128
K2 = 4 * WB
NS = 16
MB = 1 << 20
COST = 10 ** 6
BF = jnp.bfloat16
F32 = jnp.float32
NT = (((1,), (1,)), ((), ()))


def shift(x, axis, step, size):
    return lax.ppermute(x, axis, [(k, (k + step) % size) for k in range(size)])


def pick_kernel(place_ref, spec_hbm, valid_ref, out_ref, spec_ref, raw_ref, sems):
    def fetch(g):
        bins = pl.ds(g * 16, 16)
        return pltpu.make_async_copy(spec_hbm.at[:, bins], spec_ref.at[:, bins], sems.at[g])

    for g in range(8):
        fetch(g).start()
    lane = lax.broadcasted_iota(jnp.int32, (8, CH), 1)
    row = lax.broadcasted_iota(jnp.int32, (8, CH), 0)
    hit = jnp.zeros((8, CH), F32)
    for k in range(4):
        hit = jnp.where((row == k) & (lane == place_ref[k]), 1.0, hit)
    onehot = hit.astype(BF)
    own_first = pl.multiple_of(place_ref[4] * WB, 8)

    def block(g, acc):
        fetch(g).wait()
        for j in range(8):
            k = 8 * g + j
            rows = jnp.concatenate([spec_ref[p, 2 * k + odd] for odd in range(2) for p in range(2)], axis=0)
            raw = lax.dot_general(onehot, rows, NT, preferred_element_type=F32)
            raw_ref[k] = raw
            acc = acc + raw * raw
        return acc

    acc = lax.fori_loop(0, 8, block, jnp.zeros((8, K2), F32))
    total = acc[:, 0:WB] + acc[:, WB:2 * WB] + acc[:, 2 * WB:3 * WB] + acc[:, 3 * WB:]
    picked_all = lax.dot_general(onehot, valid_ref[...].astype(BF), NT, preferred_element_type=F32)
    picked_own = lax.dot_general(onehot, valid_ref[pl.ds(own_first, WB), :].astype(BF), NT, preferred_element_type=F32)
    scale = picked_own / jnp.sqrt(total * (1.0 / F) + 1e-6)
    scale4 = jnp.concatenate([scale] * 4, axis=1)

    @pl.loop(0, F2)
    def _(k):
        out_ref[k] = (raw_ref[k] * scale4)[:4].astype(BF)

    out_ref[F2] = picked_all[:4].astype(BF)


VM = pl.BlockSpec(memory_space=pltpu.VMEM)


def pick(place, spectra, valid):
    return pl.pallas_call(
        pick_kernel,
        in_specs=[pl.BlockSpec(memory_space=pltpu.SMEM), pl.BlockSpec(memory_space=pltpu.HBM), VM],
        out_specs=VM,
        out_shape=jax.ShapeDtypeStruct((F2 + 1, 4, K2), BF),
        scratch_shapes=[pltpu.VMEM((2, F, WB, CH), BF), pltpu.VMEM((F2, 8, K2), F32), pltpu.SemaphoreType.DMA((8,))],
        compiler_params=pltpu.CompilerParams(vmem_limit_bytes=58 * MB),
        cost_estimate=pl.CostEstimate(flops=2 * 10 ** 9, bytes_accessed=7 * 10 ** 6, transcendentals=0),
        name="pick_sources",
    )(place, spectra, valid)


def whiten_kernel(spec_ref, valid_ref, out_ref):
    @pl.loop(0, WB // 16)
    def _(g):
        rows = pl.ds(pl.multiple_of(g * 16, 16), 16)

        def power(g, energy):
            for f in range(16):
                re = spec_ref[0, g * 16 + f, rows].astype(F32)
                im = spec_ref[1, g * 16 + f, rows].astype(F32)
                energy = energy + (re * re + im * im)
            return energy

        energy = lax.fori_loop(0, F // 16, power, jnp.zeros((16, CH), F32))
        scale = valid_ref[rows].astype(F32) / jnp.sqrt(energy * (1.0 / F) + 1e-6)

        @pl.loop(0, F // 16)
        def _(g):
            for f in range(16):
                for p in range(2):
                    out_ref[p, g * 16 + f, rows] = (spec_ref[p, g * 16 + f, rows].astype(F32) * scale).astype(BF)


def whiten(spectra, own_valid):
    return pl.pallas_call(
        whiten_kernel,
        in_specs=[VM, VM],
        out_specs=VM,
        out_shape=pltpu.VMEM((2, F, WB, CH), BF),
        compiler_params=pltpu.CompilerParams(vmem_limit_bytes=16 * MB),
        cost_estimate=pl.CostEstimate(flops=10 ** 6, bytes_accessed=10 ** 5, transcendentals=0),
        name="whiten_channels",
    )(spectra, own_valid)


def cross_kernel(n_ring, n_side, *refs):
    n_chunks = n_ring + n_side
    parts = refs[:n_chunks]
    valids = refs[n_chunks:2 * n_chunks]
    chan_ref, valid_ref, table_ref, keep_ref, send_ref, cnt_ref, x_ref = refs[2 * n_chunks:]
    step = pl.program_id(0)
    n = n_chunks * NS
    pad = jnp.zeros((256 - 2 * WB, 2 * CH), BF)
    held = []
    for k in range(8):
        lhs = jnp.concatenate([part[k] for part in parts], axis=0)
        for odd in range(2):
            re = chan_ref[0, step * 16 + 2 * k + odd]
            im = chan_ref[1, step * 16 + 2 * k + odd]
            top = jnp.concatenate([re, im], axis=1)
            low = jnp.concatenate([im, -re], axis=1)
            if odd:
                rhs = jnp.concatenate([pad, top, low], axis=0)
                used = lhs[:, 128:]
            else:
                rhs = jnp.concatenate([top, low, pad], axis=0)
                used = lhs[:, :256]
            both = jnp.dot(used, rhs, preferred_element_type=F32)
            held.append(both.astype(BF))
    for p in range(2):
        block = jnp.stack([h[:, p * CH:(p + 1) * CH] for h in held])
        first_bin = pl.multiple_of(p * F + step * 16, 16)
        x_ref[:, pl.ds(first_bin, 16), :] = jnp.transpose(block, (1, 0, 2))

    @pl.when(step == 7)
    def _():
        for c in range(n_chunks):
            cnt_ref[c * NS:(c + 1) * NS] = jnp.dot(valids[c][0], valid_ref[...], preferred_element_type=F32)
        table = table_ref[...]

        def pair(out_ref, slot, row):
            lag = jnp.dot(table, jnp.concatenate([x_ref[row], x_ref[row + 1]], axis=1), preferred_element_type=F32)
            out_ref[slot] = lag[:, :CH].astype(BF)
            out_ref[slot + 1] = lag[:, CH:].astype(BF)

        for block, (out_ref, half) in enumerate(((keep_ref, 0), (keep_ref, 1), (send_ref, 0), (send_ref, 1))):
            for c in range(n_ring):
                for q in range(0, NS // 4, 2):
                    pair(out_ref, half * (n_ring * 4) + c * 4 + q, c * NS + block * 4 + q)

        if n_side:
            for q in range(0, n_side * NS, 2):
                pair(send_ref, n_ring * 8 + q, n_ring * NS + q)


def cross(ring, side, chan, valid, table):
    chunks = list(ring) + list(side)
    n_ring, n_side, n_chunks = len(ring), len(side), len(chunks)
    n = n_chunks * NS
    part = pl.BlockSpec((8, NS, K2), lambda i: (i, 0, 0))
    tail = pl.BlockSpec((1, NS, K2), lambda i: (F2, 0, 0))
    sizes = [n_ring * 8, n_ring * 8 + n_side * NS]
    return pl.pallas_call(
        functools.partial(cross_kernel, n_ring, n_side),
        grid=(8,),
        in_specs=[part] * n_chunks + [tail] * n_chunks + [
            VM,
            pl.BlockSpec((W, CH), lambda i: (0, 0)),
            pl.BlockSpec((L, 2 * F), lambda i: (0, 0)),
        ],
        out_specs=[pl.BlockSpec((k, L, CH), lambda i: (0, 0, 0)) for k in sizes] + [pl.BlockSpec((n, CH), lambda i: (0, 0))],
        out_shape=[jax.ShapeDtypeStruct((k, L, CH), BF) for k in sizes] + [jax.ShapeDtypeStruct((n, CH), F32)],
        scratch_shapes=[pltpu.VMEM((n, 2 * F, CH), BF)],
        compiler_params=pltpu.CompilerParams(vmem_limit_bytes=24 * MB),
        cost_estimate=pl.CostEstimate(flops=COST * n_chunks, bytes_accessed=10 ** 5 * n_chunks, transcendentals=0),
        name="cross_lag",
    )(*chunks, *chunks, chan, valid, table)


def finish_kernel(rows_ref, live_ref, bounds_ref, *refs):
    n_in = len(refs) - 2
    lag_ref, peak_ref = refs[n_in], refs[n_in + 1]
    lag_index = lax.broadcasted_iota(jnp.int32, (L, CH), 0)
    first = 0
    for g in range(n_in // 3):
        keep_ref, recv_ref, cnt_ref = refs[3 * g], refs[3 * g + 1], refs[3 * g + 2]
        count = recv_ref.shape[0]

        def one(r, keep_ref=keep_ref, recv_ref=recv_ref, cnt_ref=cnt_ref, first=first):
            row = rows_ref[first + r]
            total = keep_ref[r].astype(F32) + recv_ref[r].astype(F32)
            value = (total / cnt_ref[pl.ds(r, 1), :]).astype(BF)
            lag_ref[row] = value.T
            lower = bounds_ref[0, pl.ds(row, 1), :]
            upper = bounds_ref[1, pl.ds(row, 1), :]
            inside = (lag_index >= lower) & (lag_index < upper)
            best = jnp.max(jnp.where(inside, value.astype(F32), -jnp.inf), axis=0, keepdims=True)
            peak_ref[pl.ds(row, 1), :] = best

        @pl.when(live_ref[g] != 0)
        def _(one=one, count=count):
            @pl.loop(0, count // 4)
            def _(q):
                for k in range(4):
                    one(q * 4 + k)
        first += count


def finish(rows, live, bounds2, groups):
    flat = [x for g in groups for x in g]
    smem = pl.BlockSpec(memory_space=pltpu.SMEM)
    return pl.pallas_call(
        finish_kernel,
        in_specs=[smem, smem] + [VM] * (1 + len(flat)),
        out_specs=[VM, VM],
        out_shape=[jax.ShapeDtypeStruct((64, CH, L), BF), jax.ShapeDtypeStruct((64, CH), F32)],
        compiler_params=pltpu.CompilerParams(vmem_limit_bytes=24 * MB),
        cost_estimate=pl.CostEstimate(flops=10 ** 7, bytes_accessed=8 * 10 ** 6, transcendentals=0),
        name="finish_lags",
    )(rows, live, bounds2, *flat)


def lag_table():
    bins_col = (1 + jnp.arange(F, dtype=jnp.int32))[:, None]
    lag_row = jnp.arange(L, dtype=jnp.int32)[None, :] - L // 2
    angles = (bins_col * lag_row % (2 * F)).astype(F32) * (2.0 * math.pi / (2 * F))
    cos, sin = jnp.cos(angles).astype(BF), jnp.sin(angles).astype(BF)
    return jnp.concatenate([cos, -sin], axis=0).T


def tie(values):
    return lax.optimization_barrier(values)


def add(a, b):
    return (a.astype(F32) + b.astype(F32)).astype(BF)


def local(spectra, valid, sources, bounds):
    xlo = lax.axis_index("xlo")
    core = lax.axis_index("core")
    y = lax.axis_index("y")
    xh = lax.axis_index("xh")
    z = lax.axis_index("z")
    freq = xlo * 2 + core
    offsets = sources - ((y * 2 + xh) * 8 + z) * CH
    place = jnp.concatenate([offsets, freq[None].astype(jnp.int32)])
    valid_b = valid.astype(BF)
    own_valid = lax.dynamic_slice_in_dim(valid_b, freq * WB, WB, 0)
    table = lag_table()

    picked = pick(place, spectra, valid)
    other = shift(picked, "xh", 1, 2)
    mine1 = jnp.concatenate([picked[:, :2], other[:, :2]], axis=1)
    mine2 = jnp.concatenate([picked[:, 2:], other[:, 2:]], axis=1)

    def swap_core(keep, send):
        got = shift(send, "core", 1, 2)
        n, half = keep.shape[0], keep.shape[0] // 2
        side = add(send[n:], got[n:]) if send.shape[0] > n else None
        return add(keep[:half], got[:half]), add(keep[half:], got[half:n]), side

    def swap_x(mine, away):
        return mine, shift(away, "xlo", 1, 2)

    def side_x(total, odd, low_is_mine):
        half = total.shape[0] // 2
        pairs = [((h * 2 + c) * 4 + k, ((1 - h) * 2 + c) * 4 + k)
                 for k in range(4) for c in range(2) for h in range(2) if c == (k + odd) % 2]
        mine = jnp.where(low_is_mine, total[:half], total[half:])
        away = jnp.where(low_is_mine, total[half:], total[:half])
        return mine, lax.ppermute(away, ("xlo", "core", "y"), pairs)

    r = (freq - y) % 4
    halves = ((0, 1, -1, 2), (-2, 3, -3, 4))

    def lanes(ks, first):
        return [(k, e, first + j) for k in ks for e in range(2) for j in range(2)]

    spots = []
    for ks in ((0, 1, -1), (2, -2), (3, -3, 4)):
        spots += lanes(ks, 0)
    spots += lanes(halves[0], 2) + lanes(halves[1], 2)
    one = spots + lanes(halves[0], 2) + lanes(halves[1], 2)
    two = spots + lanes(halves[1], 2) + lanes(halves[0], 2)
    tables = np.array([one, two], np.int32)
    spot = jnp.where(r == 1, tables[0], tables[1])
    rows = ((xh ^ spot[:, 1]) * 32 + ((z + spot[:, 0]) % 8) * 4 + spot[:, 2]).astype(jnp.int32)
    even = 1 - r % 2
    live = jnp.where(np.arange(6) < 3, 1, jnp.where(np.arange(6) == 3, even, 1 - even)).astype(jnp.int32)
    bounds2 = jnp.stack([bounds[:, :, 0], bounds[:, :, 1]])

    r1 = (shift(mine1, "y", -1, 4), shift(mine1, "y", 2, 4), shift(mine1, "y", 1, 4))
    b1, bm1 = shift(mine2, "z", -1, 8), shift(mine2, "z", 1, 8)
    b2, bm2 = shift(b1, "z", -1, 8), shift(bm1, "z", 1, 8)
    b3, bm3 = shift(b2, "z", -1, 8), shift(bm2, "z", 1, 8)
    up, far, down = r1
    by_y = jnp.stack([mine1, up, far, down])
    order = [lax.dynamic_index_in_dim(by_y, ((freq ^ m) - y) % 4, 0, keepdims=False) for m in (0, 2, 1, 3)]
    a0 = jnp.concatenate(order, axis=1)
    h0 = [jnp.concatenate([mine2, b1, bm1, b2], axis=1)]
    a0, h0, bm2, b3, bm3, rows, live = tie((a0, h0, bm2, b3, bm3, rows, live))
    chan = whiten(spectra, own_valid)

    def run(ring, side=(), after=()):
        gated = tie((table,) + tuple(after))[0] if after else table
        return cross(ring, side, chan, valid_b, gated)

    a1, am1 = shift(a0, "z", -1, 8), shift(a0, "z", 1, 8)
    h0.append(shift(h0[0], "y", -1, 4))
    b4 = shift(b3, "z", -1, 8)
    h1 = [jnp.concatenate([bm2, b3, bm3, b4], axis=1)]
    h1.append(shift(h1[0], "y", 1, 4))
    a1, am1, h0, h1, chan = tie((a1, am1, h0, h1, chan))
    a2, am2 = shift(a1, "z", -1, 8), shift(am1, "z", 1, 8)
    h0.append(shift(h0[1], "y", -1, 4))
    h1.append(shift(h1[1], "y", 1, 4))
    keep1, send1, cnt1 = run([a0, a1, am1], [h0[1], h1[1]])
    a2, am2, h0, h1, keep1, send1 = tie((a2, am2, h0, h1, keep1, send1))
    a3, am3 = shift(a2, "z", -1, 8), shift(am2, "z", 1, 8)
    h0.append(shift(h0[2], "y", -1, 4))
    h1.append(shift(h1[2], "y", 1, 4))
    mine1, away1, side1 = swap_core(keep1, send1)
    keep2, send2, cnt2 = run([a2, am2], [h0[0], h1[0], h0[2], h1[2]], (side1,))
    k1 = swap_x(mine1, away1)
    a3, am3, h0, h1, k1, side1, keep2, send2 = tie((a3, am3, h0, h1, k1, side1, keep2, send2))
    p1 = side_x(side1, 1, r == 1)
    mine2, away2, side2 = swap_core(keep2, send2)
    cut = F2 // 2
    a4 = jnp.concatenate([shift(am3[:cut], "z", 1, 8), shift(a3[cut:], "z", -1, 8)], axis=0)
    a4, p1, mine2, away2, side2 = tie((a4, p1, mine2, away2, side2))
    p0 = side_x(side2, 0, r == 0)
    k2 = swap_x(mine2, away2)
    keep3, send3, cnt3 = run([a3, am3, a4], [h0[3], h1[3]])
    mine3, away3, side3 = swap_core(keep3, send3)
    p3 = side_x(side3, 1, r == 3)
    k3 = swap_x(mine3, away3)

    groups = []
    for ks, (mine, recv), cnt in ((3, k1, cnt1), (2, k2, cnt2), (3, k3, cnt3)):
        groups.append((mine, recv, jnp.concatenate([cnt[c * NS:c * NS + 4] for c in range(ks)], axis=0)))
    cnt1, cnt2, cnt3 = cnt1[3 * NS:], cnt2[2 * NS:], cnt3[3 * NS:]
    groups.append((*p0, jnp.where(r == 0, cnt2[:2 * NS], cnt2[2 * NS:])))
    groups.append((*p1, jnp.where(r == 1, cnt1[:NS], cnt1[NS:])))
    groups.append((*p3, jnp.where(r == 3, cnt3[:NS], cnt3[NS:])))
    lag_corr, peak = finish(rows, live, bounds2, groups)
    return (lag_corr, peak)


def solution(mesh):
    fine = Mesh(mesh.devices.reshape(2, 2, 4, 2, 8), ("xlo", "core", "y", "xh", "z"))
    freq, rcv = ("xlo", "core"), ("y", "xh", "z")
    in_specs = (P(None, None, freq, rcv), P(None, rcv), P(rcv), P(freq, rcv, None))
    out_specs = (P(freq, rcv, None), P(freq, rcv))
    return jax.shard_map(local, mesh=fine, in_specs=in_specs, out_specs=out_specs, check_vma=False)
```

```python
import functools
import math

import jax
import jax.numpy as jnp
import numpy as np
from jax import lax
from jax.experimental import pallas as pl
from jax.experimental.pallas import tpu as pltpu
from jax.sharding import Mesh, PartitionSpec as P

F = 128
F2 = F // 2
L = 128
W = 384
WB = 96
CH = 128
K2 = 4 * WB
NS = 16
MB = 1 << 20
COST = 10 ** 6
BF = jnp.bfloat16
F32 = jnp.float32
NT = (((1,), (1,)), ((), ()))


def shift(x, axis, step, size):
    return lax.ppermute(x, axis, [(k, (k + step) % size) for k in range(size)])


def pick_kernel(place_ref, spec_hbm, valid_ref, out_ref, spec_ref, raw_ref, sems):
    def fetch(g):
        bins = pl.ds(g * 16, 16)
        return pltpu.make_async_copy(spec_hbm.at[:, bins], spec_ref.at[:, bins], sems.at[g])

    for g in range(8):
        fetch(g).start()
    lane = lax.broadcasted_iota(jnp.int32, (8, CH), 1)
    row = lax.broadcasted_iota(jnp.int32, (8, CH), 0)
    hit = jnp.zeros((8, CH), F32)
    for k in range(4):
        hit = jnp.where((row == k) & (lane == place_ref[k]), 1.0, hit)
    onehot = hit.astype(BF)
    own_first = pl.multiple_of(place_ref[4] * WB, 8)

    def block(g, acc):
        fetch(g).wait()
        for j in range(8):
            k = 8 * g + j
            rows = jnp.concatenate([spec_ref[p, 2 * k + odd] for odd in range(2) for p in range(2)], axis=0)
            raw = lax.dot_general(onehot, rows, NT, preferred_element_type=F32)
            raw_ref[k] = raw
            acc = acc + raw * raw
        return acc

    acc = lax.fori_loop(0, 8, block, jnp.zeros((8, K2), F32))
    total = acc[:, 0:WB] + acc[:, WB:2 * WB] + acc[:, 2 * WB:3 * WB] + acc[:, 3 * WB:]
    picked_all = lax.dot_general(onehot, valid_ref[...].astype(BF), NT, preferred_element_type=F32)
    picked_own = lax.dot_general(onehot, valid_ref[pl.ds(own_first, WB), :].astype(BF), NT, preferred_element_type=F32)
    scale = picked_own / jnp.sqrt(total * (1.0 / F) + 1e-6)
    scale4 = jnp.concatenate([scale] * 4, axis=1)

    @pl.loop(0, F2)
    def _(k):
        out_ref[k] = (raw_ref[k] * scale4)[:4].astype(BF)

    out_ref[F2] = picked_all[:4].astype(BF)


VM = pl.BlockSpec(memory_space=pltpu.VMEM)


def pick(place, spectra, valid):
    return pl.pallas_call(
        pick_kernel,
        in_specs=[pl.BlockSpec(memory_space=pltpu.SMEM), pl.BlockSpec(memory_space=pltpu.HBM), VM],
        out_specs=VM,
        out_shape=jax.ShapeDtypeStruct((F2 + 1, 4, K2), BF),
        scratch_shapes=[pltpu.VMEM((2, F, WB, CH), BF), pltpu.VMEM((F2, 8, K2), F32), pltpu.SemaphoreType.DMA((8,))],
        compiler_params=pltpu.CompilerParams(vmem_limit_bytes=58 * MB),
        cost_estimate=pl.CostEstimate(flops=2 * 10 ** 9, bytes_accessed=7 * 10 ** 6, transcendentals=0),
        name="pick_sources",
    )(place, spectra, valid)


def whiten_kernel(spec_ref, valid_ref, out_ref):
    @pl.loop(0, WB // 16)
    def _(g):
        rows = pl.ds(pl.multiple_of(g * 16, 16), 16)

        def power(g, energy):
            for f in range(16):
                re = spec_ref[0, g * 16 + f, rows].astype(F32)
                im = spec_ref[1, g * 16 + f, rows].astype(F32)
                energy = energy + (re * re + im * im)
            return energy

        energy = lax.fori_loop(0, F // 16, power, jnp.zeros((16, CH), F32))
        scale = valid_ref[rows].astype(F32) / jnp.sqrt(energy * (1.0 / F) + 1e-6)

        @pl.loop(0, F // 16)
        def _(g):
            for f in range(16):
                for p in range(2):
                    out_ref[p, g * 16 + f, rows] = (spec_ref[p, g * 16 + f, rows].astype(F32) * scale).astype(BF)


def whiten(spectra, own_valid):
    return pl.pallas_call(
        whiten_kernel,
        in_specs=[VM, VM],
        out_specs=VM,
        out_shape=pltpu.VMEM((2, F, WB, CH), BF),
        compiler_params=pltpu.CompilerParams(vmem_limit_bytes=16 * MB),
        cost_estimate=pl.CostEstimate(flops=10 ** 6, bytes_accessed=10 ** 5, transcendentals=0),
        name="whiten_channels",
    )(spectra, own_valid)


def cross_kernel(n_ring, n_side, *refs):
    n_chunks = n_ring + n_side
    parts = refs[:n_chunks]
    valids = refs[n_chunks:2 * n_chunks]
    chan_ref, valid_ref, table_ref, keep_ref, send_ref, cnt_ref, x_ref = refs[2 * n_chunks:]
    step = pl.program_id(0)
    n = n_chunks * NS
    pad = jnp.zeros((256 - 2 * WB, 2 * CH), BF)
    held = []
    for k in range(8):
        lhs = jnp.concatenate([part[k] for part in parts], axis=0)
        for odd in range(2):
            re = chan_ref[0, step * 16 + 2 * k + odd]
            im = chan_ref[1, step * 16 + 2 * k + odd]
            top = jnp.concatenate([re, im], axis=1)
            low = jnp.concatenate([im, -re], axis=1)
            if odd:
                rhs = jnp.concatenate([pad, top, low], axis=0)
                used = lhs[:, 128:]
            else:
                rhs = jnp.concatenate([top, low, pad], axis=0)
                used = lhs[:, :256]
            both = jnp.dot(used, rhs, preferred_element_type=F32)
            held.append(both.astype(BF))
    for p in range(2):
        block = jnp.stack([h[:, p * CH:(p + 1) * CH] for h in held])
        first_bin = pl.multiple_of(p * F + step * 16, 16)
        x_ref[:, pl.ds(first_bin, 16), :] = jnp.transpose(block, (1, 0, 2))

    @pl.when(step == 7)
    def _():
        for c in range(n_chunks):
            cnt_ref[c * NS:(c + 1) * NS] = jnp.dot(valids[c][0], valid_ref[...], preferred_element_type=F32)
        table = table_ref[...]

        def pair(out_ref, slot, row):
            lag = jnp.dot(table, jnp.concatenate([x_ref[row], x_ref[row + 1]], axis=1), preferred_element_type=F32)
            out_ref[slot] = lag[:, :CH].astype(BF)
            out_ref[slot + 1] = lag[:, CH:].astype(BF)

        for block, (out_ref, half) in enumerate(((keep_ref, 0), (keep_ref, 1), (send_ref, 0), (send_ref, 1))):
            for c in range(n_ring):
                for q in range(0, NS // 4, 2):
                    pair(out_ref, half * (n_ring * 4) + c * 4 + q, c * NS + block * 4 + q)

        if n_side:
            for q in range(0, n_side * NS, 2):
                pair(send_ref, n_ring * 8 + q, n_ring * NS + q)


def cross(ring, side, chan, valid, table):
    chunks = list(ring) + list(side)
    n_ring, n_side, n_chunks = len(ring), len(side), len(chunks)
    n = n_chunks * NS
    part = pl.BlockSpec((8, NS, K2), lambda i: (i, 0, 0))
    tail = pl.BlockSpec((1, NS, K2), lambda i: (F2, 0, 0))
    sizes = [n_ring * 8, n_ring * 8 + n_side * NS]
    return pl.pallas_call(
        functools.partial(cross_kernel, n_ring, n_side),
        grid=(8,),
        in_specs=[part] * n_chunks + [tail] * n_chunks + [
            VM,
            pl.BlockSpec((W, CH), lambda i: (0, 0)),
            pl.BlockSpec((L, 2 * F), lambda i: (0, 0)),
        ],
        out_specs=[pl.BlockSpec((k, L, CH), lambda i: (0, 0, 0)) for k in sizes] + [pl.BlockSpec((n, CH), lambda i: (0, 0))],
        out_shape=[jax.ShapeDtypeStruct((k, L, CH), BF) for k in sizes] + [jax.ShapeDtypeStruct((n, CH), F32)],
        scratch_shapes=[pltpu.VMEM((n, 2 * F, CH), BF)],
        compiler_params=pltpu.CompilerParams(vmem_limit_bytes=24 * MB),
        cost_estimate=pl.CostEstimate(flops=COST * n_chunks, bytes_accessed=10 ** 5 * n_chunks, transcendentals=0),
        name="cross_lag",
    )(*chunks, *chunks, chan, valid, table)


def finish_kernel(rows_ref, live_ref, bounds_ref, *refs):
    n_in = len(refs) - 2
    lag_ref, peak_ref = refs[n_in], refs[n_in + 1]
    lag_index = lax.broadcasted_iota(jnp.int32, (L, CH), 0)
    first = 0
    for g in range(n_in // 3):
        keep_ref, recv_ref, cnt_ref = refs[3 * g], refs[3 * g + 1], refs[3 * g + 2]
        count = recv_ref.shape[0]

        def one(r, keep_ref=keep_ref, recv_ref=recv_ref, cnt_ref=cnt_ref, first=first):
            row = rows_ref[first + r]
            total = keep_ref[r].astype(F32) + recv_ref[r].astype(F32)
            value = (total / cnt_ref[pl.ds(r, 1), :]).astype(BF)
            lag_ref[row] = value.T
            lower = bounds_ref[0, pl.ds(row, 1), :]
            upper = bounds_ref[1, pl.ds(row, 1), :]
            inside = (lag_index >= lower) & (lag_index < upper)
            best = jnp.max(jnp.where(inside, value.astype(F32), -jnp.inf), axis=0, keepdims=True)
            peak_ref[pl.ds(row, 1), :] = best

        @pl.when(live_ref[g] != 0)
        def _(one=one, count=count):
            @pl.loop(0, count // 4)
            def _(q):
                for k in range(4):
                    one(q * 4 + k)
        first += count


def finish(rows, live, bounds2, groups):
    flat = [x for g in groups for x in g]
    smem = pl.BlockSpec(memory_space=pltpu.SMEM)
    return pl.pallas_call(
        finish_kernel,
        in_specs=[smem, smem] + [VM] * (1 + len(flat)),
        out_specs=[VM, VM],
        out_shape=[jax.ShapeDtypeStruct((64, CH, L), BF), jax.ShapeDtypeStruct((64, CH), F32)],
        compiler_params=pltpu.CompilerParams(vmem_limit_bytes=24 * MB),
        cost_estimate=pl.CostEstimate(flops=10 ** 7, bytes_accessed=8 * 10 ** 6, transcendentals=0),
        name="finish_lags",
    )(rows, live, bounds2, *flat)


def lag_table():
    bins_col = (1 + jnp.arange(F, dtype=jnp.int32))[:, None]
    lag_row = jnp.arange(L, dtype=jnp.int32)[None, :] - L // 2
    angles = (bins_col * lag_row % (2 * F)).astype(F32) * (2.0 * math.pi / (2 * F))
    cos, sin = jnp.cos(angles).astype(BF), jnp.sin(angles).astype(BF)
    return jnp.concatenate([cos, -sin], axis=0).T


def tie(values):
    return lax.optimization_barrier(values)


def add(a, b):
    return (a.astype(F32) + b.astype(F32)).astype(BF)


def local(spectra, valid, sources, bounds):
    xlo = lax.axis_index("xlo")
    core = lax.axis_index("core")
    y = lax.axis_index("y")
    xh = lax.axis_index("xh")
    z = lax.axis_index("z")
    freq = xlo * 2 + core
    offsets = sources - ((y * 2 + xh) * 8 + z) * CH
    place = jnp.concatenate([offsets, freq[None].astype(jnp.int32)])
    valid_b = valid.astype(BF)
    own_valid = lax.dynamic_slice_in_dim(valid_b, freq * WB, WB, 0)
    table = lag_table()

    picked = pick(place, spectra, valid)
    other = shift(picked, "xh", 1, 2)
    mine1 = jnp.concatenate([picked[:, :2], other[:, :2]], axis=1)
    mine2 = jnp.concatenate([picked[:, 2:], other[:, 2:]], axis=1)

    def swap_core(keep, send):
        got = shift(send, "core", 1, 2)
        n, half = keep.shape[0], keep.shape[0] // 2
        side = add(send[n:], got[n:]) if send.shape[0] > n else None
        return add(keep[:half], got[:half]), add(keep[half:], got[half:n]), side

    def swap_x(mine, away):
        return mine, shift(away, "xlo", 1, 2)

    def side_x(total, odd, low_is_mine):
        half = total.shape[0] // 2
        pairs = [((h * 2 + c) * 4 + k, ((1 - h) * 2 + c) * 4 + k)
                 for k in range(4) for c in range(2) for h in range(2) if c == (k + odd) % 2]
        mine = jnp.where(low_is_mine, total[:half], total[half:])
        away = jnp.where(low_is_mine, total[half:], total[:half])
        return mine, lax.ppermute(away, ("xlo", "core", "y"), pairs)

    r = (freq - y) % 4
    halves = ((0, 1, -1, 2), (-2, 3, -3, 4))

    def lanes(ks, first):
        return [(k, e, first + j) for k in ks for e in range(2) for j in range(2)]

    spots = []
    for ks in ((0, 1, -1), (2, -2), (3, -3, 4)):
        spots += lanes(ks, 0)
    spots += lanes(halves[0], 2) + lanes(halves[1], 2)
    one = spots + lanes(halves[0], 2) + lanes(halves[1], 2)
    two = spots + lanes(halves[1], 2) + lanes(halves[0], 2)
    tables = np.array([one, two], np.int32)
    spot = jnp.where(r == 1, tables[0], tables[1])
    rows = ((xh ^ spot[:, 1]) * 32 + ((z + spot[:, 0]) % 8) * 4 + spot[:, 2]).astype(jnp.int32)
    even = 1 - r % 2
    live = jnp.where(np.arange(6) < 3, 1, jnp.where(np.arange(6) == 3, even, 1 - even)).astype(jnp.int32)
    bounds2 = jnp.stack([bounds[:, :, 0], bounds[:, :, 1]])

    r1 = (shift(mine1, "y", -1, 4), shift(mine1, "y", 2, 4), shift(mine1, "y", 1, 4))
    b1, bm1 = shift(mine2, "z", -1, 8), shift(mine2, "z", 1, 8)
    b2, bm2 = shift(b1, "z", -1, 8), shift(bm1, "z", 1, 8)
    b3, bm3 = shift(b2, "z", -1, 8), shift(bm2, "z", 1, 8)
    up, far, down = r1
    by_y = jnp.stack([mine1, up, far, down])
    order = [lax.dynamic_index_in_dim(by_y, ((freq ^ m) - y) % 4, 0, keepdims=False) for m in (0, 2, 1, 3)]
    a0 = jnp.concatenate(order, axis=1)
    h0 = [jnp.concatenate([mine2, b1, bm1, b2], axis=1)]
    a0, h0, bm2, b3, bm3, rows, live = tie((a0, h0, bm2, b3, bm3, rows, live))
    chan = whiten(spectra, own_valid)

    def run(ring, side=(), after=()):
        gated = tie((table,) + tuple(after))[0] if after else table
        return cross(ring, side, chan, valid_b, gated)

    a1, am1 = shift(a0, "z", -1, 8), shift(a0, "z", 1, 8)
    h0.append(shift(h0[0], "y", -1, 4))
    b4 = shift(b3, "z", -1, 8)
    h1 = [jnp.concatenate([bm2, b3, bm3, b4], axis=1)]
    h1.append(shift(h1[0], "y", 1, 4))
    a1, am1, h0, h1, chan = tie((a1, am1, h0, h1, chan))
    a2, am2 = shift(a1, "z", -1, 8), shift(am1, "z", 1, 8)
    h0.append(shift(h0[1], "y", -1, 4))
    h1.append(shift(h1[1], "y", 1, 4))
    keep1, send1, cnt1 = run([a0, a1, am1], [h0[1], h1[1]])
    a2, am2, h0, h1, keep1, send1 = tie((a2, am2, h0, h1, keep1, send1))
    a3, am3 = shift(a2, "z", -1, 8), shift(am2, "z", 1, 8)
    h0.append(shift(h0[2], "y", -1, 4))
    h1.append(shift(h1[2], "y", 1, 4))
    mine1, away1, side1 = swap_core(keep1, send1)
    keep2, send2, cnt2 = run([a2, am2], [h0[0], h1[0], h0[2], h1[2]], (side1,))
    k1 = swap_x(mine1, away1)
    a3, am3, h0, h1, k1, side1, keep2, send2 = tie((a3, am3, h0, h1, k1, side1, keep2, send2))
    p1 = side_x(side1, 1, r == 1)
    mine2, away2, side2 = swap_core(keep2, send2)
    cut = F2 // 2
    a4 = jnp.concatenate([shift(am3[:cut], "z", 1, 8), shift(a3[cut:], "z", -1, 8)], axis=0)
    k2 = swap_x(mine2, away2)
    a4, p1, k2, side2 = tie((a4, p1, k2, side2))
    p0 = side_x(side2, 0, r == 0)
    keep3, send3, cnt3 = run([a3, am3, a4], [h0[3], h1[3]])
    mine3, away3, side3 = swap_core(keep3, send3)
    p3 = side_x(side3, 1, r == 3)
    k3 = swap_x(mine3, away3)

    groups = []
    for ks, (mine, recv), cnt in ((3, k1, cnt1), (2, k2, cnt2), (3, k3, cnt3)):
        groups.append((mine, recv, jnp.concatenate([cnt[c * NS:c * NS + 4] for c in range(ks)], axis=0)))
    cnt1, cnt2, cnt3 = cnt1[3 * NS:], cnt2[2 * NS:], cnt3[3 * NS:]
    groups.append((*p0, jnp.where(r == 0, cnt2[:2 * NS], cnt2[2 * NS:])))
    groups.append((*p1, jnp.where(r == 1, cnt1[:NS], cnt1[NS:])))
    groups.append((*p3, jnp.where(r == 3, cnt3[:NS], cnt3[NS:])))
    lag_corr, peak = finish(rows, live, bounds2, groups)
    return (lag_corr, peak)


def solution(mesh):
    fine = Mesh(mesh.devices.reshape(2, 2, 4, 2, 8), ("xlo", "core", "y", "xh", "z"))
    freq, rcv = ("xlo", "core"), ("y", "xh", "z")
    in_specs = (P(None, None, freq, rcv), P(None, rcv), P(rcv), P(freq, rcv, None))
    out_specs = (P(freq, rcv, None), P(freq, rcv))
    return jax.shard_map(local, mesh=fine, in_specs=in_specs, out_specs=out_specs, check_vma=False)
```
